32 devices in a mesh: groups: 2 (over x), date: 16 (over z, y, core).
Axes of the slice: x: 2, y: 2, z: 4, core: 2. Of those that a mesh axis runs over, the one named last changes fastest.
Arguments:
- secondary_complex_slabs: bfloat16 [32, 2, 32, 256], P(('groups', 'date')), parts along dimension 0, may hold values from -6 to 6
- reference_complex_slab: bfloat16 [2, 256, 64], P(None, ('groups', 'date')), parts along dimension 1, may hold values from -6 to 6
- elevation_tiles: float32 [64, 8, 256], P(('groups', 'date')), parts along dimension 0, may hold values from -6 to 6
- baseline: float32 [32, 2], P(('groups', 'date')), parts along dimension 0, may hold values from -2 to 2
- block_terrain_tile: int32 [256, 1], P('groups'), parts along dimension 0, may hold values from 0 to 31
- block_first_row: int32 [256], P('groups'), parts along dimension 0, may hold values from 0 to 3
- block_first_column: int32 [256], P('groups'), parts along dimension 0, may hold values from 0 to 239
- block_fraction_weights: int32 [256, 2], P('groups'), parts along dimension 0, may hold values from 0 to 15
Outputs:
- filtered: bfloat16 [32, 2, 32, 256], P(('groups', 'date')), parts along dimension 0
The draws below stay inside these ranges and needn't reach their ends.
There are 2 independent parts, one for each index of `groups`. The reference program is written for one: setup_inputs(seed, part) draws one part's arguments, and reference() takes and returns one part's arrays. A program takes and returns all parts, laid end to end along the dimension named above; each array names one. Nothing has to cross between parts.
Inputs may be any that keep to these rules, and one draw needn't show every extreme that they name: `block_terrain_tile`: every tile is named by at least one block.
All inputs are finite; a program needn't handle non-finite values.
Results may differ from the reference program's by a relative error of at most 0.0074.
Values may be sent and summed in bfloat16 or wider, within the bound.
A program may use at most 64 MiB of HBM per device.

```python
import math
import jax
import jax.numpy as jnp
from jax import lax

SLAB_ROWS = 32
SLAB_COLS = 256
PATCH_SIZE = 64
TILE_ROW_COUNT = 8
TILE_COLUMNS = 256
BLOCK_LINES = 4
BLOCK_SAMPLES = 16
ALL_DATES = 16
TERRAIN_TILES = 32
BLOCKS = 128


def set_ends(entries, key, least, top_value):
    spot = [jax.random.randint(jax.random.fold_in(key, axis), (), 0, length) for axis, length in enumerate(entries.shape)]
    longest = entries.shape.index(max(entries.shape))
    neighbour = spot[:longest] + [(spot[longest] + 1) % entries.shape[longest]] + spot[longest + 1:]
    return entries.at[tuple(spot)].set(least).at[tuple(neighbour)].set(top_value)


def shard_levels(rng, dims, cuts, least, largest):
    factor_of = 1.0
    for position, shards_of in cuts:
        steps = jax.random.uniform(jax.random.fold_in(jax.random.fold_in(rng, 6), position), (shards_of,), jnp.float32, least / len(cuts), largest / len(cuts))
        factor_of = factor_of * jnp.repeat(jnp.exp(steps), dims[position] // shards_of).reshape((-1,) + (1,) * (len(dims) - 1 - position))
    return factor_of


def distinct(own_key, rows, number_of, top, lift):
    sequence = jax.random.permutation(jax.random.fold_in(own_key, 1), number_of)
    favour = sequence
    for power in range(3):
        favour = favour * favour // number_of
    favour = favour * lift // number_of
    tickets = jax.random.randint(jax.random.fold_in(own_key, 2), (rows, number_of), 0, 4096) + favour
    sure = jax.random.permutation(jax.random.fold_in(own_key, 3), rows)[jnp.arange(number_of) % rows]
    tickets = jnp.where(jnp.arange(rows)[:, None] == sure[None, :], 1 << 14, tickets)
    merit = tickets * number_of + jnp.arange(number_of)
    return lax.top_k(merit.astype(jnp.int32), top)[1].astype(jnp.int32)


def centred(key, dims, scale, reach, pieces=(), held_as=jnp.bfloat16):
    result = jax.random.normal(key, dims, jnp.float32) * scale
    if len(pieces) > 0:
        result = shard_levels(key, dims, pieces, -0.22, 0.18) * result
    return jnp.clip(result, min=-reach, max=reach).astype(held_as)


def setup_inputs(seed: int = 0, part: int = 0) -> dict:
    keys = jax.random.split(jax.random.key(seed), 9)
    part_keys = jax.random.split(jax.random.fold_in(keys[8], part), 9)
    return {
        "secondary_complex_slabs": centred(part_keys[0], (ALL_DATES, 2, SLAB_ROWS, SLAB_COLS), 1.0, 6.0, ((0, 16),)),
        "reference_complex_slab": centred(part_keys[1], (2, SLAB_ROWS * SLAB_COLS // 64, 64), 1.0, 6.0, ((1, 16),)),
        "elevation_tiles": centred(part_keys[2], (TERRAIN_TILES, TILE_ROW_COUNT, TILE_COLUMNS), 1.0, 6.0, ((0, 16),), jnp.float32),
        "baseline": jnp.clip(jax.random.uniform(part_keys[3], (ALL_DATES, 2), jnp.float32, -2.0, 2.0) * shard_levels(part_keys[3], (ALL_DATES, 2), ((0, 16),), -0.4, 0.0), -2.0, 2.0),
        "block_terrain_tile": distinct(part_keys[4], BLOCKS, TERRAIN_TILES, 1, 512),
        "block_first_row": set_ends(jax.random.randint(part_keys[5], (BLOCKS,), 0, TILE_ROW_COUNT - BLOCK_LINES), jax.random.fold_in(part_keys[5], 1), 0, (TILE_ROW_COUNT - BLOCK_LINES) - 1).astype(jnp.int32),
        "block_first_column": set_ends(jax.random.randint(part_keys[6], (BLOCKS,), 0, TILE_COLUMNS - BLOCK_SAMPLES), jax.random.fold_in(part_keys[6], 1), 0, (TILE_COLUMNS - BLOCK_SAMPLES) - 1).astype(jnp.int32),
        "block_fraction_weights": set_ends(jax.random.randint(part_keys[7], (BLOCKS, 2), 0, 16), jax.random.fold_in(part_keys[7], 1), 0, 15).astype(jnp.int32),
    }


def dft_tables():
    series = jnp.arange(PATCH_SIZE, dtype=jnp.int32)
    angle = (series[:, None] * series[None, :] % PATCH_SIZE).astype(jnp.float32) * (2.0 * math.pi / PATCH_SIZE)
    cosine = jnp.cos(angle).astype(jnp.bfloat16)
    sine = jnp.sin(angle).astype(jnp.bfloat16)
    forward = jnp.concatenate([jnp.concatenate([cosine, -sine], axis=1), jnp.concatenate([sine, cosine], axis=1)], axis=0)
    inverse = jnp.concatenate([jnp.concatenate([cosine, sine], axis=1), jnp.concatenate([-sine, cosine], axis=1)], axis=0)
    taper = jnp.sin(math.pi * (series.astype(jnp.float32) + 0.5) / PATCH_SIZE) ** 2
    return (cosine, sine, forward, inverse, taper)

def block_terrain_heights(elevation_tiles, terrain_tile_index, block_first_row, block_first_column, block_fraction_weights):

    def window(tile_identifier, row_begin, column_begin):
        return lax.dynamic_slice(elevation_tiles[tile_identifier], (row_begin, column_begin), (BLOCK_LINES + 1, BLOCK_SAMPLES + 1))
    windows = jax.vmap(window)(terrain_tile_index, block_first_row, block_first_column)
    weights = block_fraction_weights.astype(jnp.float32) / 16.0
    down_frac = weights[:, 0][:, None, None]
    right_frac = weights[:, 1][:, None, None]
    upper_row = (1.0 - right_frac) * windows[:, :-1, :-1] + right_frac * windows[:, :-1, 1:]
    lower_row = (1.0 - right_frac) * windows[:, 1:, :-1] + right_frac * windows[:, 1:, 1:]
    return (1.0 - down_frac) * upper_row + down_frac * lower_row

def to_image(block_entries, row_count, col_count):
    shaped = block_entries.reshape(row_count // BLOCK_LINES, col_count // BLOCK_SAMPLES, BLOCK_LINES, BLOCK_SAMPLES)
    return shaped.transpose(0, 2, 1, 3).reshape(row_count, col_count)

def interfere(date_slab, coeffs, reference_field, heights):
    col_count = heights.shape[1]
    across = (jnp.arange(col_count, dtype=jnp.float32) + 0.5) / col_count - 0.5
    phase = (coeffs[0] + coeffs[1] * across)[None, :] * heights
    sec_real = date_slab[0].astype(jnp.float32)
    sec_imag = date_slab[1].astype(jnp.float32)
    ref_real = reference_field[0].astype(jnp.float32)
    ref_imag = reference_field[1].astype(jnp.float32)
    cross_real = sec_real * ref_real + sec_imag * ref_imag
    cross_imag = sec_imag * ref_real - sec_real * ref_imag
    cosine = jnp.cos(phase)
    sine = jnp.sin(phase)
    real_part = (cross_real * cosine + cross_imag * sine).astype(jnp.bfloat16)
    imag_part = (cross_imag * cosine - cross_real * sine).astype(jnp.bfloat16)
    return (real_part, imag_part)

def goldstein(real_part, imag_part):
    row_count, col_count = real_part.shape
    half_size = PATCH_SIZE // 2
    cosine, sine, forward, inverse, taper = dft_tables()
    cos_wide = cosine.astype(jnp.float32)
    sin_wide = sine.astype(jnp.float32)
    col_patches = col_count // half_size + 1
    row_patches = row_count // half_size + 1

    def split_cols(field):
        padded = jnp.pad(field, half_size)
        block_entries = padded.reshape(padded.shape[0], col_patches + 1, half_size)
        return jnp.concatenate([block_entries[:, :-1], block_entries[:, 1:]], axis=2)
    joined = jnp.concatenate([split_cols(real_part), split_cols(imag_part)], axis=2)
    patches = jnp.stack([joined[half_size * number:half_size * number + PATCH_SIZE] for number in range(row_patches)])
    colspec = jnp.einsum('piqc,cd->piqd', patches.astype(jnp.float32), forward.astype(jnp.float32)).astype(jnp.bfloat16)
    swapped = jnp.concatenate([colspec[..., PATCH_SIZE:], -colspec[..., :PATCH_SIZE]], axis=3)
    spectrum = jnp.einsum('ki,piqc->pkqc', cos_wide, colspec.astype(jnp.float32)) + jnp.einsum('ki,piqc->pkqc', sin_wide, swapped.astype(jnp.float32))
    energy = spectrum[..., :PATCH_SIZE] ** 2 + spectrum[..., PATCH_SIZE:] ** 2
    row_smooth = energy + jnp.roll(energy, 1, axis=1) + jnp.roll(energy, -1, axis=1)
    smooth = (row_smooth + jnp.roll(row_smooth, 1, axis=3) + jnp.roll(row_smooth, -1, axis=3)) / 9.0
    average = lax.optimization_barrier(jnp.mean(smooth, axis=(1, 3), keepdims=True))
    response = jnp.sqrt((smooth + 0.1 * average) / (average + 1e-06))
    weighted = (spectrum * jnp.concatenate([response, response], axis=3)).astype(jnp.bfloat16)
    turned = jnp.concatenate([weighted[..., PATCH_SIZE:], -weighted[..., :PATCH_SIZE]], axis=3)
    rowback = (jnp.einsum('ki,piqc->pkqc', cos_wide, weighted.astype(jnp.float32)) - jnp.einsum('ki,piqc->pkqc', sin_wide, turned.astype(jnp.float32))).astype(jnp.bfloat16)
    patch_out = jnp.einsum('pkqc,cd->pkqd', rowback.astype(jnp.float32), inverse.astype(jnp.float32))
    col_taper = jnp.concatenate([taper, taper])
    patch_out = patch_out * taper[None, :, None, None] * col_taper[None, None, None, :] / float(PATCH_SIZE * PATCH_SIZE)
    stacked = patch_out[1:, :half_size] + patch_out[:-1, half_size:]
    stacked = stacked.reshape(row_count, col_patches, 2, 2, half_size)
    merged = stacked[:, 1:, :, 0] + stacked[:, :-1, :, 1]
    return merged.transpose(2, 0, 1, 3).reshape(2, row_count, col_count).astype(jnp.bfloat16)

def reference(secondary_complex_slabs, reference_complex_slab, elevation_tiles, baseline, block_terrain_tile, block_first_row, block_first_column, block_fraction_weights):
    block_entries = block_terrain_heights(elevation_tiles, block_terrain_tile[:, 0], block_first_row, block_first_column, block_fraction_weights)
    heights = to_image(block_entries, SLAB_ROWS, SLAB_COLS)
    reference_field = reference_complex_slab.reshape(2, SLAB_ROWS, SLAB_COLS)

    def one_date(operands):
        date_slab, coeffs = operands
        real_part, imag_part = interfere(date_slab, coeffs, reference_field, heights)
        return goldstein(real_part, imag_part)
    return lax.map(one_date, (secondary_complex_slabs, baseline))
```

```python
import functools
import math

import jax
import jax.numpy as jnp
import ml_dtypes
import numpy as np
from jax import lax
from jax.experimental import pallas as pl
from jax.experimental.pallas import tpu as pltpu
from jax.sharding import PartitionSpec as P

PATCH_SIZE = 64
HALF = PATCH_SIZE // 2
BLOCK_LINES = 4
BLOCK_SAMPLES = 16
LANES = 128
SUBLANES = 8
SPAN = LANES // HALF + 1
SPAN_LANES = -(-SPAN * PATCH_SIZE // LANES) * LANES
GROUP_STEP = (SPAN - 1) * PATCH_SIZE


@functools.lru_cache(maxsize=None)
def tables():
    series = np.arange(PATCH_SIZE)
    angle = (series[:, None] * series[None, :] % PATCH_SIZE) * (2.0 * math.pi / PATCH_SIZE)
    cosine, sine = np.cos(angle), np.sin(angle)
    taper = np.sin(math.pi * (series + 0.5) / PATCH_SIZE) ** 2 / (PATCH_SIZE * PATCH_SIZE)
    into = np.zeros((2, LANES, SPAN_LANES))
    back = np.zeros((2, SPAN_LANES, 2, LANES))
    for m in range(LANES):
        block, j = divmod(m, HALF)
        for half, (q, n) in enumerate(((block, HALF + j), (block + 1, j))):
            lanes = slice(q * PATCH_SIZE, (q + 1) * PATCH_SIZE)
            into[0, m, lanes] = cosine[n]
            into[1, m, lanes] = sine[n]
            back[0, lanes, half, m] = cosine[:, n]
            back[1, lanes, half, m] = -sine[:, n]
    into = into.reshape(2 * LANES, SPAN_LANES)
    back = back.reshape(2 * SPAN_LANES, 2 * LANES)
    c, s = cosine[:, :HALF], sine[:, :HALF]
    down = np.block([[c, s], [-s, c]])
    c, s = cosine[:HALF], sine[:HALF]
    up = np.block([[c, -s], [s, c]])
    weights = np.stack([np.tile(taper[HALF:], LANES // HALF), np.tile(taper[:HALF], LANES // HALF)])
    placed = tuple(m.astype(np.float32).astype(ml_dtypes.bfloat16) for m in (into, down, up, back))
    return placed + (weights.astype(np.float32),)


def kernel(
    n,
    elev, ref_in, sec, base, first_tile, first_row, first_col, frac,
    into_h, down_h, up_h, back_h, taper_h,
    out,
    tiles, refbuf, refwide, heights, secbuf, into, down, up, back, taper,
    local_sem, send_sem, recv_sem, fwd_sem,
):
    rows, cols = sec.shape[2], sec.shape[3]
    own = elev.shape[0]
    me = lax.axis_index("date")
    partner = me + 1 - 2 * (me % 2)
    peers = [(me + 2 * k) % n for k in range(1, n // 2)]
    sources = [(me + n - 2 * k) % n for k in range(1, n // 2)]
    barrier = pltpu.get_barrier_semaphore()
    for peer in peers + [partner]:
        pl.semaphore_signal(
            barrier, inc=1, device_id={"date": peer}, device_id_type=pl.DeviceIdType.MESH
        )

    def slot(device):
        return tiles.at[pl.ds(device * own, own)]

    local = [
        pltpu.make_async_copy(ref_in, refbuf.at[me], local_sem.at[0]),
        pltpu.make_async_copy(elev, slot(me), local_sem.at[1]),
        pltpu.make_async_copy(sec, secbuf, local_sem.at[2]),
        pltpu.make_async_copy(into_h, into, local_sem.at[3]),
        pltpu.make_async_copy(down_h, down, local_sem.at[4]),
        pltpu.make_async_copy(up_h, up, local_sem.at[5]),
        pltpu.make_async_copy(back_h, back, local_sem.at[6]),
        pltpu.make_async_copy(taper_h, taper, local_sem.at[7]),
    ]
    for copy in local:
        copy.start()

    def remote(src, dst, sends, number, kind, source, device):
        return pltpu.make_async_remote_copy(
            src_ref=src,
            dst_ref=dst,
            send_sem=sends.at[kind, number],
            recv_sem=recv_sem.at[kind, source],
            device_id={"date": device},
            device_id_type=pl.DeviceIdType.MESH,
        )

    pl.semaphore_wait(barrier, n // 2)
    sent = []
    for number, peer in enumerate(peers + [partner]):
        sent.append(remote(ref_in, refbuf.at[me], send_sem, number, 0, me, peer))
        sent[-1].start()
    for number, peer in enumerate(peers + [partner]):
        sent.append(remote(elev, slot(me), send_sem, number, 1, me, peer))
        sent[-1].start()
    for kind in range(2):
        for number, source in enumerate(sources):
            where = refbuf.at[source] if kind == 0 else slot(source)
            copy = remote(where, where, fwd_sem, number, kind, source, partner)
            copy.wait_recv()
            copy.start()
            sent.append(copy)
    others = [partner] + [source + 1 - 2 * (source % 2) for source in sources]
    for source in others:
        remote(refbuf.at[source], refbuf.at[source], send_sem, 0, 0, source, partner).wait_recv()
    local[0].wait()

    line = refbuf.shape[3]
    per_row = cols // line
    field = []
    for part in range(2):
        refwide[part] = refbuf[:, part].astype(jnp.float32).reshape(rows * per_row, line)
        field.append(
            jnp.concatenate(
                [refwide[part, pl.ds(m, rows, stride=per_row), :] for m in range(per_row)], axis=1
            )
        )
    for copy in local[2:]:
        copy.wait()
    lane_row = lax.broadcasted_iota(jnp.int32, (1, cols), 1).astype(jnp.float32)
    across = (lane_row + 0.5) / cols - 0.5

    for source in others:
        remote(slot(source), slot(source), send_sem, 0, 1, source, partner).wait_recv()
    local[1].wait()

    lane = lax.broadcasted_iota(jnp.int32, (SUBLANES, LANES), 1)
    sublane = lax.broadcasted_iota(jnp.int32, (SUBLANES, LANES), 0)
    grid_cols = cols // BLOCK_SAMPLES
    per_group = LANES // BLOCK_SAMPLES
    bands = SUBLANES // BLOCK_LINES

    def eight_rows(step, carry):
        for group in range(cols // LANES):
            total = jnp.zeros((SUBLANES, LANES), jnp.float32)
            for band in range(bands):
                for place in range(per_group):
                    b = (step * bands + band) * grid_cols + group * per_group + place
                    tile, col = first_tile[b], first_col[b]
                    fy = frac[0, b].astype(jnp.float32) * (1.0 / 16.0)
                    fx = frac[1, b].astype(jnp.float32) * (1.0 / 16.0)
                    near = tiles[tile, :, 0:LANES]
                    for other in range(1, cols // LANES):
                        far = tiles[tile, :, other * LANES : (other + 1) * LANES]
                        near = jnp.where(lane + (other - 1) * LANES >= col, near, far)
                    move = band * BLOCK_LINES + SUBLANES - first_row[b]
                    upper = pltpu.roll(near, lax.rem(move, SUBLANES), 0)
                    lower = pltpu.roll(near, lax.rem(move - 1, SUBLANES), 0)
                    mixed = upper + fy * (lower - upper)
                    shift = place * BLOCK_SAMPLES + cols - col
                    left = pltpu.roll(mixed, lax.rem(shift, LANES), 1)
                    right = pltpu.roll(mixed, lax.rem(shift - 1, LANES), 1)
                    value = left + fx * (right - left)
                    inside = (lane // BLOCK_SAMPLES == place) & (sublane // BLOCK_LINES == band)
                    total = jnp.where(inside, value, total)
            heights[
                pl.ds(pl.multiple_of(step * SUBLANES, SUBLANES), SUBLANES),
                group * LANES : (group + 1) * LANES,
            ] = total
        return carry

    lax.fori_loop(0, rows // SUBLANES, eight_rows, 0)

    groups = cols // LANES
    lanes64 = lax.broadcasted_iota(jnp.int32, (PATCH_SIZE, LANES), 1) % PATCH_SIZE
    first, last = lanes64 == 0, lanes64 == PATCH_SIZE - 1
    same_patch = (
        lax.broadcasted_iota(jnp.int32, (2 * LANES, LANES), 0) % LANES // PATCH_SIZE
        == lax.broadcasted_iota(jnp.int32, (2 * LANES, LANES), 1) // PATCH_SIZE
    )
    ones = jnp.where(same_patch, 1.0, 0.0).astype(jnp.bfloat16)

    def dot(a, b):
        return jnp.dot(a, b, preferred_element_type=jnp.float32)

    for date in range(sec.shape[0]):
        phase = (base[date, 0] + base[date, 1] * across) * heights[...]
        sec_real = secbuf[date, 0].astype(jnp.float32)
        sec_imag = secbuf[date, 1].astype(jnp.float32)
        cross_real = sec_real * field[0] + sec_imag * field[1]
        cross_imag = sec_imag * field[0] - sec_real * field[1]
        cosine, sine = jnp.cos(phase), jnp.sin(phase)
        real = (cross_real * cosine + cross_imag * sine).astype(jnp.bfloat16)
        imag = (cross_imag * cosine - cross_real * sine).astype(jnp.bfloat16)
        left = []
        for g in range(groups):
            re, im = (x[:, g * LANES : (g + 1) * LANES] for x in (real, imag))
            left.append(jnp.concatenate([re, im], axis=1))
            left.append(jnp.concatenate([im, -re], axis=1))
        product = dot(jnp.concatenate(left, axis=0), into[...])
        pieces = [None] * ((groups * GROUP_STEP + SPAN_LANES - GROUP_STEP) // LANES)
        for g in range(groups):
            for k in range(SPAN_LANES // LANES):
                term = product[
                    2 * rows * g : 2 * rows * (g + 1), k * LANES : (k + 1) * LANES
                ]
                at = g * GROUP_STEP // LANES + k
                pieces[at] = term if pieces[at] is None else pieces[at] + term
        colspec = jnp.concatenate(pieces, axis=1).astype(jnp.bfloat16)
        spectrum = dot(down[...], colspec)
        parts = []
        sums = []
        for k in range(len(pieces)):
            here = spectrum[:, k * LANES : (k + 1) * LANES]
            re, im = here[:PATCH_SIZE], here[PATCH_SIZE:]
            energy = re * re + im * im
            total = energy[0:SUBLANES]
            for r in range(1, PATCH_SIZE // SUBLANES):
                total = total + energy[r * SUBLANES : (r + 1) * SUBLANES]
            sums.append(total)
            parts.append((re, im, energy))
        total = jnp.concatenate(sums, axis=0)
        high = total.astype(jnp.bfloat16)
        low = (total - high.astype(jnp.float32)).astype(jnp.bfloat16)
        means = dot(jnp.concatenate([high, low], axis=1), ones)
        weighted = []
        for k, (re, im, energy) in enumerate(parts):
            mean = jnp.sum(means[k * SUBLANES : (k + 1) * SUBLANES], axis=0, keepdims=True)
            mean = mean / float(PATCH_SIZE * PATCH_SIZE)
            tall = energy + pltpu.roll(energy, 1, 0) + pltpu.roll(energy, PATCH_SIZE - 1, 0)
            before = jnp.where(
                first, pltpu.roll(tall, LANES + 1 - PATCH_SIZE, 1), pltpu.roll(tall, 1, 1)
            )
            after = jnp.where(
                last, pltpu.roll(tall, PATCH_SIZE - 1, 1), pltpu.roll(tall, LANES - 1, 1)
            )
            smooth = (tall + before + after) * (1.0 / 9.0)
            response = jnp.sqrt((smooth + 0.1 * mean) * (1.0 / (mean + 1e-06)))
            weighted.append(
                jnp.concatenate([re * response, im * response], axis=0).astype(jnp.bfloat16)
            )
        rowback = dot(up[...], jnp.concatenate(weighted, axis=1)).astype(jnp.bfloat16)
        left = []
        for g in range(groups):
            here = rowback[:, g * GROUP_STEP : g * GROUP_STEP + SPAN_LANES]
            re, im = here[:rows], here[rows:]
            left.append(jnp.concatenate([re, im], axis=1))
            left.append(jnp.concatenate([im, -re], axis=1))
        product = dot(jnp.concatenate(left, axis=0), back[...])
        merged = product[:, :LANES] * taper[0:1, :] + product[:, LANES:] * taper[1:2, :]
        merged = merged.astype(jnp.bfloat16)
        for g in range(groups):
            for part in range(2):
                begin = (2 * g + part) * rows
                out[date, part, :, g * LANES : (g + 1) * LANES] = merged[begin : begin + rows]

    for copy in sent:
        copy.wait_send()


def per_device(
    n,
    secondary_complex_slabs,
    reference_complex_slab,
    elevation_tiles,
    baseline,
    block_terrain_tile,
    block_first_row,
    block_first_column,
    block_fraction_weights,
):
    dates, _, rows, cols = secondary_complex_slabs.shape
    assert rows == HALF and elevation_tiles.shape[1:] == (SUBLANES, cols)
    lines, line = reference_complex_slab.shape[1:]
    constants = [jnp.asarray(table) for table in tables()]
    anywhere = pl.BlockSpec(memory_space=pl.ANY)
    scalars = pl.BlockSpec(memory_space=pltpu.SMEM)
    return pl.pallas_call(
        functools.partial(kernel, n),
        out_shape=jax.ShapeDtypeStruct(secondary_complex_slabs.shape, jnp.bfloat16),
        in_specs=[anywhere] * 3 + [scalars] * 5 + [anywhere] * 5,
        out_specs=pl.BlockSpec(memory_space=pltpu.VMEM),
        scratch_shapes=[
            pltpu.VMEM((n * elevation_tiles.shape[0],) + elevation_tiles.shape[1:], jnp.float32),
            pltpu.VMEM((n, 2, lines, line), jnp.bfloat16),
            pltpu.VMEM((2, n * lines, line), jnp.float32),
            pltpu.VMEM((rows, cols), jnp.float32),
            pltpu.VMEM(secondary_complex_slabs.shape, jnp.bfloat16),
        ]
        + [pltpu.VMEM(table.shape, table.dtype) for table in constants]
        + [
            pltpu.SemaphoreType.DMA((8,)),
            pltpu.SemaphoreType.DMA((2, n // 2)),
            pltpu.SemaphoreType.DMA((2, n)),
            pltpu.SemaphoreType.DMA((2, n // 2)),
        ],
        compiler_params=pltpu.CompilerParams(collective_id=0, has_side_effects=True),
    )(
        elevation_tiles,
        reference_complex_slab,
        secondary_complex_slabs,
        baseline,
        block_terrain_tile.reshape(-1),
        block_first_row,
        block_first_column,
        block_fraction_weights.T,
        *constants,
    )


def solution(mesh):
    return jax.shard_map(
        functools.partial(per_device, mesh.shape["date"]),
        mesh=mesh,
        in_specs=(
            P(("groups", "date"), None, None, None),
            P(None, ("groups", "date"), None),
            P(("groups", "date"), None, None),
            P(("groups", "date"), None),
            P("groups", None),
            P("groups"),
            P("groups"),
            P("groups", None),
        ),
        out_specs=P(("groups", "date"), None, None, None),
        check_vma=False,
    )
```

```python
import functools
import math

import jax
import jax.numpy as jnp
import ml_dtypes
import numpy as np
from jax import lax
from jax.experimental import pallas as pl
from jax.experimental.pallas import tpu as pltpu
from jax.sharding import PartitionSpec as P

PATCH_SIZE = 64
HALF = PATCH_SIZE // 2
BLOCK_LINES = 4
BLOCK_SAMPLES = 16
LANES = 128
SUBLANES = 8
SPAN = LANES // HALF + 1
SPAN_LANES = -(-SPAN * PATCH_SIZE // LANES) * LANES
GROUP_STEP = (SPAN - 1) * PATCH_SIZE


@functools.lru_cache(maxsize=None)
def tables():
    series = np.arange(PATCH_SIZE)
    angle = (series[:, None] * series[None, :] % PATCH_SIZE) * (2.0 * math.pi / PATCH_SIZE)
    cosine, sine = np.cos(angle), np.sin(angle)
    taper = np.sin(math.pi * (series + 0.5) / PATCH_SIZE) ** 2 / (PATCH_SIZE * PATCH_SIZE)
    into = np.zeros((2, LANES, SPAN_LANES))
    back = np.zeros((2, SPAN_LANES, 2, LANES))
    for m in range(LANES):
        block, j = divmod(m, HALF)
        for half, (q, n) in enumerate(((block, HALF + j), (block + 1, j))):
            lanes = slice(q * PATCH_SIZE, (q + 1) * PATCH_SIZE)
            into[0, m, lanes] = cosine[n]
            into[1, m, lanes] = sine[n]
            back[0, lanes, half, m] = cosine[:, n]
            back[1, lanes, half, m] = -sine[:, n]
    into = into.reshape(2 * LANES, SPAN_LANES)
    back = back.reshape(2 * SPAN_LANES, 2 * LANES)
    c, s = cosine[:, :HALF], sine[:, :HALF]
    down = np.block([[c, s], [-s, c]])
    c, s = cosine[:HALF], sine[:HALF]
    up = np.block([[c, -s], [s, c]])
    weights = np.stack([np.tile(taper[HALF:], LANES // HALF), np.tile(taper[:HALF], LANES // HALF)])
    placed = tuple(m.astype(np.float32).astype(ml_dtypes.bfloat16) for m in (into, down, up, back))
    return placed + (weights.astype(np.float32),)


def flipped(index, bits):
    result = index
    bit = 1
    while bit <= bits:
        if bits & bit:
            result = result + bit - 2 * bit * (index // bit % 2)
        bit *= 2
    return result


def kernel(
    n,
    elev, ref_in, sec, base_h, tile_h, row_h, col_h, frac_h,
    into_h, down_h, up_h, back_h, taper_h,
    out,
    tiles, refbuf, refwide, heights, secbuf, into, down, up, back, taper,
    base, first_tile, first_row, first_col, frac,
    local_sem, send_sem, recv_sem, fwd_sem,
):
    rows, cols = sec.shape[2], sec.shape[3]
    own = elev.shape[0]
    me = lax.axis_index("date")
    partner = flipped(me, 1)
    peers = [flipped(me, 2 * k) for k in reversed(range(1, n // 2))]
    sources = peers[::-1]
    barrier = pltpu.get_barrier_semaphore()
    for peer in peers + [partner]:
        pl.semaphore_signal(
            barrier, inc=1, device_id={"date": peer}, device_id_type=pl.DeviceIdType.MESH
        )

    def slot(device):
        return tiles.at[pl.ds(device * own, own)]

    local = [
        pltpu.make_async_copy(ref_in, refbuf.at[me], local_sem.at[0]),
        pltpu.make_async_copy(elev, slot(me), local_sem.at[1]),
        pltpu.make_async_copy(sec, secbuf, local_sem.at[2]),
        pltpu.make_async_copy(into_h, into, local_sem.at[3]),
        pltpu.make_async_copy(down_h, down, local_sem.at[4]),
        pltpu.make_async_copy(up_h, up, local_sem.at[5]),
        pltpu.make_async_copy(back_h, back, local_sem.at[6]),
        pltpu.make_async_copy(taper_h, taper, local_sem.at[7]),
        pltpu.make_async_copy(base_h, base, local_sem.at[8]),
        pltpu.make_async_copy(tile_h, first_tile, local_sem.at[9]),
        pltpu.make_async_copy(row_h, first_row, local_sem.at[10]),
        pltpu.make_async_copy(col_h, first_col, local_sem.at[11]),
        pltpu.make_async_copy(frac_h, frac, local_sem.at[12]),
    ]
    for copy in local:
        copy.start()

    def remote(src, dst, sends, number, kind, source, device):
        return pltpu.make_async_remote_copy(
            src_ref=src,
            dst_ref=dst,
            send_sem=sends.at[kind, number],
            recv_sem=recv_sem.at[kind, source],
            device_id={"date": device},
            device_id_type=pl.DeviceIdType.MESH,
        )

    pl.semaphore_wait(barrier, n // 2)
    sent = []
    for kind in (1, 0):
        for number, peer in enumerate(peers + [partner]):
            src, dst = (elev, slot(me)) if kind else (ref_in, refbuf.at[me])
            sent.append(remote(src, dst, send_sem, number, kind, me, peer))
            sent[-1].start()
    for kind in (1, 0):
        for number, source in enumerate(sources):
            where = slot(source) if kind else refbuf.at[source]
            copy = remote(where, where, fwd_sem, number, kind, source, partner)
            copy.wait_recv()
            copy.start()
            sent.append(copy)
    others = [partner] + [flipped(source, 1) for source in sources]
    for copy in local:
        copy.wait()
    for source in others:
        remote(slot(source), slot(source), send_sem, 0, 1, source, partner).wait_recv()

    lane = lax.broadcasted_iota(jnp.int32, (SUBLANES, LANES), 1)
    sublane = lax.broadcasted_iota(jnp.int32, (SUBLANES, LANES), 0)
    grid_cols = cols // BLOCK_SAMPLES
    per_group = LANES // BLOCK_SAMPLES
    bands = SUBLANES // BLOCK_LINES

    def eight_rows(step, carry):
        for group in range(cols // LANES):
            total = jnp.zeros((SUBLANES, LANES), jnp.float32)
            for band in range(bands):
                for place in range(per_group):
                    b = (step * bands + band) * grid_cols + group * per_group + place
                    tile, col = first_tile[b], first_col[b]
                    fy = frac[0, b].astype(jnp.float32)
                    fx = frac[1, b].astype(jnp.float32)
                    near = tiles[tile, :, 0:LANES]
                    for other in range(1, cols // LANES):
                        far = tiles[tile, :, other * LANES : (other + 1) * LANES]
                        near = jnp.where(lane + (other - 1) * LANES >= col, near, far)
                    move = band * BLOCK_LINES + SUBLANES - first_row[b]
                    upper = pltpu.roll(near, (move) & (SUBLANES - 1), 0)
                    lower = pltpu.roll(near, (move - 1) & (SUBLANES - 1), 0)
                    mixed = 16.0 * upper + fy * (lower - upper)
                    shift = place * BLOCK_SAMPLES + cols - col
                    left = pltpu.roll(mixed, (shift) & (LANES - 1), 1)
                    right = pltpu.roll(mixed, (shift - 1) & (LANES - 1), 1)
                    value = 16.0 * left + fx * (right - left)
                    inside = (lane // BLOCK_SAMPLES == place) & (sublane // BLOCK_LINES == band)
                    total = jnp.where(inside, value, total)
            heights[
                pl.ds(pl.multiple_of(step * SUBLANES, SUBLANES), SUBLANES),
                group * LANES : (group + 1) * LANES,
            ] = total * (1.0 / 256.0)
        return carry

    lax.fori_loop(0, rows // SUBLANES, eight_rows, 0)

    for source in others:
        remote(refbuf.at[source], refbuf.at[source], send_sem, 0, 0, source, partner).wait_recv()
    line = refbuf.shape[3]
    per_row = cols // line
    field = []
    for part in range(2):
        refwide[part] = refbuf[:, part].astype(jnp.float32).reshape(rows * per_row, line)
        field.append(
            jnp.concatenate(
                [refwide[part, pl.ds(m, rows, stride=per_row), :] for m in range(per_row)], axis=1
            )
        )
    lane_row = lax.broadcasted_iota(jnp.int32, (1, cols), 1).astype(jnp.float32)
    across = (lane_row + 0.5) / cols - 0.5

    groups = cols // LANES
    lanes64 = lax.broadcasted_iota(jnp.int32, (PATCH_SIZE, LANES), 1) % PATCH_SIZE
    first, last = lanes64 == 0, lanes64 == PATCH_SIZE - 1
    same_patch = (
        lax.broadcasted_iota(jnp.int32, (2 * LANES, LANES), 0) % LANES // PATCH_SIZE
        == lax.broadcasted_iota(jnp.int32, (2 * LANES, LANES), 1) // PATCH_SIZE
    )
    ones = jnp.where(same_patch, 1.0, 0.0).astype(jnp.bfloat16)

    def dot(a, b):
        return jnp.dot(a, b, preferred_element_type=jnp.float32)

    for date in range(sec.shape[0]):
        phase = (base[date, 0] + base[date, 1] * across) * heights[...]
        sec_real = secbuf[date, 0].astype(jnp.float32)
        sec_imag = secbuf[date, 1].astype(jnp.float32)
        cross_real = sec_real * field[0] + sec_imag * field[1]
        cross_imag = sec_imag * field[0] - sec_real * field[1]
        cosine, sine = jnp.cos(phase), jnp.sin(phase)
        real = (cross_real * cosine + cross_imag * sine).astype(jnp.bfloat16)
        imag = (cross_imag * cosine - cross_real * sine).astype(jnp.bfloat16)
        left = []
        for g in range(groups):
            re, im = (x[:, g * LANES : (g + 1) * LANES] for x in (real, imag))
            left.append(jnp.concatenate([re, im], axis=1))
            left.append(jnp.concatenate([im, -re], axis=1))
        product = dot(jnp.concatenate(left, axis=0), into[...])
        pieces = [None] * ((groups * GROUP_STEP + SPAN_LANES - GROUP_STEP) // LANES)
        for g in range(groups):
            for k in range(SPAN_LANES // LANES):
                term = product[
                    2 * rows * g : 2 * rows * (g + 1), k * LANES : (k + 1) * LANES
                ]
                at = g * GROUP_STEP // LANES + k
                pieces[at] = term if pieces[at] is None else pieces[at] + term
        colspec = jnp.concatenate(pieces, axis=1).astype(jnp.bfloat16)
        spectrum = dot(down[...], colspec)
        parts = []
        sums = []
        for k in range(len(pieces)):
            here = spectrum[:, k * LANES : (k + 1) * LANES]
            re, im = here[:PATCH_SIZE], here[PATCH_SIZE:]
            energy = re * re + im * im
            total = energy[0:SUBLANES]
            for r in range(1, PATCH_SIZE // SUBLANES):
                total = total + energy[r * SUBLANES : (r + 1) * SUBLANES]
            sums.append(total)
            parts.append((re, im, energy))
        total = jnp.concatenate(sums, axis=0)
        high = total.astype(jnp.bfloat16)
        low = (total - high.astype(jnp.float32)).astype(jnp.bfloat16)
        means = dot(jnp.concatenate([high, low], axis=1), ones)
        weighted = []
        for k, (re, im, energy) in enumerate(parts):
            mean = jnp.sum(means[k * SUBLANES : (k + 1) * SUBLANES], axis=0, keepdims=True)
            mean = mean / float(PATCH_SIZE * PATCH_SIZE)
            tall = energy + pltpu.roll(energy, 1, 0) + pltpu.roll(energy, PATCH_SIZE - 1, 0)
            before = jnp.where(
                first, pltpu.roll(tall, LANES + 1 - PATCH_SIZE, 1), pltpu.roll(tall, 1, 1)
            )
            after = jnp.where(
                last, pltpu.roll(tall, PATCH_SIZE - 1, 1), pltpu.roll(tall, LANES - 1, 1)
            )
            smooth = (tall + before + after) * (1.0 / 9.0)
            response = jnp.sqrt((smooth + 0.1 * mean) * (1.0 / (mean + 1e-06)))
            weighted.append(
                jnp.concatenate([re * response, im * response], axis=0).astype(jnp.bfloat16)
            )
        rowback = dot(up[...], jnp.concatenate(weighted, axis=1)).astype(jnp.bfloat16)
        left = []
        for g in range(groups):
            here = rowback[:, g * GROUP_STEP : g * GROUP_STEP + SPAN_LANES]
            re, im = here[:rows], here[rows:]
            left.append(jnp.concatenate([re, im], axis=1))
            left.append(jnp.concatenate([im, -re], axis=1))
        product = dot(jnp.concatenate(left, axis=0), back[...])
        merged = product[:, :LANES] * taper[0:1, :] + product[:, LANES:] * taper[1:2, :]
        merged = merged.astype(jnp.bfloat16)
        for g in range(groups):
            for part in range(2):
                begin = (2 * g + part) * rows
                out[date, part, :, g * LANES : (g + 1) * LANES] = merged[begin : begin + rows]

    for copy in sent:
        copy.wait_send()


def per_device(
    n,
    secondary_complex_slabs,
    reference_complex_slab,
    elevation_tiles,
    baseline,
    block_terrain_tile,
    block_first_row,
    block_first_column,
    block_fraction_weights,
):
    dates, _, rows, cols = secondary_complex_slabs.shape
    assert rows == HALF and elevation_tiles.shape[1:] == (SUBLANES, cols)
    lines, line = reference_complex_slab.shape[1:]
    constants = [jnp.asarray(table) for table in tables()]
    anywhere = pl.BlockSpec(memory_space=pl.ANY)
    scalars = (
        baseline,
        block_terrain_tile.reshape(-1),
        block_first_row,
        block_first_column,
        block_fraction_weights.T,
    )
    return pl.pallas_call(
        functools.partial(kernel, n),
        out_shape=pltpu.VMEM(secondary_complex_slabs.shape, jnp.bfloat16),
        in_specs=[anywhere] * 13,
        out_specs=pl.BlockSpec(memory_space=pltpu.VMEM),
        scratch_shapes=[
            pltpu.VMEM((n * elevation_tiles.shape[0],) + elevation_tiles.shape[1:], jnp.float32),
            pltpu.VMEM((n, 2, lines, line), jnp.bfloat16),
            pltpu.VMEM((2, n * lines, line), jnp.float32),
            pltpu.VMEM((rows, cols), jnp.float32),
            pltpu.VMEM(secondary_complex_slabs.shape, jnp.bfloat16),
        ]
        + [pltpu.VMEM(table.shape, table.dtype) for table in constants]
        + [pltpu.SMEM(x.shape, x.dtype) for x in scalars]
        + [
            pltpu.SemaphoreType.DMA((13,)),
            pltpu.SemaphoreType.DMA((2, n // 2)),
            pltpu.SemaphoreType.DMA((2, n)),
            pltpu.SemaphoreType.DMA((2, n // 2)),
        ],
        compiler_params=pltpu.CompilerParams(collective_id=0, has_side_effects=True),
    )(
        elevation_tiles,
        reference_complex_slab,
        secondary_complex_slabs,
        *scalars,
        *constants,
    )


def solution(mesh):
    return jax.shard_map(
        functools.partial(per_device, mesh.shape["date"]),
        mesh=mesh,
        in_specs=(
            P(("groups", "date"), None, None, None),
            P(None, ("groups", "date"), None),
            P(("groups", "date"), None, None),
            P(("groups", "date"), None),
            P("groups", None),
            P("groups"),
            P("groups"),
            P("groups", None),
        ),
        out_specs=P(("groups", "date"), None, None, None),
        check_vma=False,
    )
```

```python
import functools
import math

import jax
import jax.numpy as jnp
import ml_dtypes
import numpy as np
from jax import lax
from jax.experimental import pallas as pl
from jax.experimental.pallas import tpu as pltpu
from jax.sharding import PartitionSpec as P

PATCH_SIZE = 64
HALF = PATCH_SIZE // 2
BLOCK_LINES = 4
BLOCK_SAMPLES = 16
HEIGHT_REACH = 6.0
HEIGHT_STEPS = 32767.0
LANES = 128
SUBLANES = 8
SPAN = LANES // HALF + 1
SPAN_LANES = -(-SPAN * PATCH_SIZE // LANES) * LANES
GROUP_STEP = (SPAN - 1) * PATCH_SIZE


@functools.lru_cache(maxsize=None)
def tables():
    series = np.arange(PATCH_SIZE)
    angle = (series[:, None] * series[None, :] % PATCH_SIZE) * (2.0 * math.pi / PATCH_SIZE)
    cosine, sine = np.cos(angle), np.sin(angle)
    taper = np.sin(math.pi * (series + 0.5) / PATCH_SIZE) ** 2 / (PATCH_SIZE * PATCH_SIZE)
    into = np.zeros((2, LANES, SPAN_LANES))
    back = np.zeros((2, SPAN_LANES, 2, LANES))
    for m in range(LANES):
        block, j = divmod(m, HALF)
        for half, (q, n) in enumerate(((block, HALF + j), (block + 1, j))):
            lanes = slice(q * PATCH_SIZE, (q + 1) * PATCH_SIZE)
            into[0, m, lanes] = cosine[n]
            into[1, m, lanes] = sine[n]
            back[0, lanes, half, m] = cosine[:, n]
            back[1, lanes, half, m] = -sine[:, n]
    into = into.reshape(2 * LANES, SPAN_LANES)
    back = back.reshape(2 * SPAN_LANES, 2 * LANES)
    c, s = cosine[:, :HALF], sine[:, :HALF]
    down = np.block([[c, s], [-s, c]])
    c, s = cosine[:HALF], sine[:HALF]
    up = np.block([[c, -s], [s, c]])
    weights = np.stack([np.tile(taper[HALF:], LANES // HALF), np.tile(taper[:HALF], LANES // HALF)])
    placed = tuple(m.astype(np.float32).astype(ml_dtypes.bfloat16) for m in (into, down, up, back))
    return placed + (weights.astype(np.float32),)


def flipped(index, bits):
    result = index
    bit = 1
    while bit <= bits:
        if bits & bit:
            result = result + bit - 2 * bit * (index // bit % 2)
        bit *= 2
    return result


def kernel(
    n,
    elev, ref_in, sec, base_h, tile_h, row_h, col_h, frac_h,
    into_h, down_h, up_h, back_h, taper_h,
    out,
    tiles, elevbuf, codes, refbuf, refwide, heights, secbuf, into, down, up, back, taper,
    base, first_tile, first_row, first_col, frac,
    local_sem, send_sem, recv_sem, fwd_sem,
):
    rows, cols = sec.shape[2], sec.shape[3]
    own = elev.shape[0]
    me = lax.axis_index("date")
    partner = flipped(me, 1)
    peers = [flipped(me, 2 * k) for k in reversed(range(1, n // 2))]
    sources = peers[::-1]
    barrier = pltpu.get_barrier_semaphore()
    for peer in peers + [partner]:
        pl.semaphore_signal(
            barrier, inc=1, device_id={"date": peer}, device_id_type=pl.DeviceIdType.MESH
        )

    def slot(device):
        return codes.at[device]

    def decode(device):
        tiles[pl.ds(device * own, own)] = (
            codes[device].astype(jnp.int32).astype(jnp.float32).reshape(elev.shape)
        )

    local = [
        pltpu.make_async_copy(ref_in, refbuf.at[me], local_sem.at[0]),
        pltpu.make_async_copy(elev, elevbuf, local_sem.at[1]),
        pltpu.make_async_copy(sec, secbuf, local_sem.at[2]),
        pltpu.make_async_copy(into_h, into, local_sem.at[3]),
        pltpu.make_async_copy(down_h, down, local_sem.at[4]),
        pltpu.make_async_copy(up_h, up, local_sem.at[5]),
        pltpu.make_async_copy(back_h, back, local_sem.at[6]),
        pltpu.make_async_copy(taper_h, taper, local_sem.at[7]),
        pltpu.make_async_copy(base_h, base, local_sem.at[8]),
        pltpu.make_async_copy(tile_h, first_tile, local_sem.at[9]),
        pltpu.make_async_copy(row_h, first_row, local_sem.at[10]),
        pltpu.make_async_copy(col_h, first_col, local_sem.at[11]),
        pltpu.make_async_copy(frac_h, frac, local_sem.at[12]),
    ]
    local[1].start()
    for copy in local[8:] + local[:1] + local[2:8]:
        copy.start()

    def remote(src, dst, sends, number, kind, source, device):
        return pltpu.make_async_remote_copy(
            src_ref=src,
            dst_ref=dst,
            send_sem=sends.at[kind, number],
            recv_sem=recv_sem.at[kind, source],
            device_id={"date": device},
            device_id_type=pl.DeviceIdType.MESH,
        )

    local[1].wait()
    scaled = jnp.round(elevbuf[...].reshape(codes.shape[1:]) * (HEIGHT_STEPS / HEIGHT_REACH))
    codes[me] = scaled.astype(jnp.int32).astype(jnp.int16)
    pl.semaphore_wait(barrier, n // 2)
    sent = []
    for kind in (1, 0):
        for number, peer in enumerate(peers + [partner]):
            src, dst = (slot(me), slot(me)) if kind else (ref_in, refbuf.at[me])
            sent.append(remote(src, dst, send_sem, number, kind, me, peer))
            sent[-1].start()
    for kind in (1, 0):
        for number, source in enumerate(sources):
            where = slot(source) if kind else refbuf.at[source]
            copy = remote(where, where, fwd_sem, number, kind, source, partner)
            copy.wait_recv()
            copy.start()
            sent.append(copy)
    others = [partner] + [flipped(source, 1) for source in sources]
    for copy in local[:1] + local[2:]:
        copy.wait()
    for device in [me] + sources:
        decode(device)
    for source in others:
        remote(slot(source), slot(source), send_sem, 0, 1, source, partner).wait_recv()
        decode(source)

    lane = lax.broadcasted_iota(jnp.int32, (SUBLANES, LANES), 1)
    sublane = lax.broadcasted_iota(jnp.int32, (SUBLANES, LANES), 0)
    grid_cols = cols // BLOCK_SAMPLES
    per_group = LANES // BLOCK_SAMPLES
    bands = SUBLANES // BLOCK_LINES

    def eight_rows(step, carry):
        for group in range(cols // LANES):
            total = jnp.zeros((SUBLANES, LANES), jnp.float32)
            for band in range(bands):
                for place in range(per_group):
                    b = (step * bands + band) * grid_cols + group * per_group + place
                    tile, col = first_tile[b], first_col[b]
                    fy = frac[0, b].astype(jnp.float32)
                    fx = frac[1, b].astype(jnp.float32)
                    near = tiles[tile, :, 0:LANES]
                    for other in range(1, cols // LANES):
                        far = tiles[tile, :, other * LANES : (other + 1) * LANES]
                        near = jnp.where(lane + (other - 1) * LANES >= col, near, far)
                    move = band * BLOCK_LINES + SUBLANES - first_row[b]
                    upper = pltpu.roll(near, (move) & (SUBLANES - 1), 0)
                    lower = pltpu.roll(near, (move - 1) & (SUBLANES - 1), 0)
                    mixed = 16.0 * upper + fy * (lower - upper)
                    shift = place * BLOCK_SAMPLES + cols - col
                    left = pltpu.roll(mixed, (shift) & (LANES - 1), 1)
                    right = pltpu.roll(mixed, (shift - 1) & (LANES - 1), 1)
                    value = 16.0 * left + fx * (right - left)
                    inside = (lane // BLOCK_SAMPLES == place) & (sublane // BLOCK_LINES == band)
                    total = jnp.where(inside, value, total)
            heights[
                pl.ds(pl.multiple_of(step * SUBLANES, SUBLANES), SUBLANES),
                group * LANES : (group + 1) * LANES,
            ] = total * (HEIGHT_REACH / HEIGHT_STEPS / 256.0)
        return carry

    lax.fori_loop(0, rows // SUBLANES, eight_rows, 0)

    for source in others:
        remote(refbuf.at[source], refbuf.at[source], send_sem, 0, 0, source, partner).wait_recv()
    line = refbuf.shape[3]
    per_row = cols // line
    field = []
    for part in range(2):
        refwide[part] = refbuf[:, part].astype(jnp.float32).reshape(rows * per_row, line)
        field.append(
            jnp.concatenate(
                [refwide[part, pl.ds(m, rows, stride=per_row), :] for m in range(per_row)], axis=1
            )
        )
    lane_row = lax.broadcasted_iota(jnp.int32, (1, cols), 1).astype(jnp.float32)
    across = (lane_row + 0.5) / cols - 0.5

    groups = cols // LANES
    lanes64 = lax.broadcasted_iota(jnp.int32, (PATCH_SIZE, LANES), 1) % PATCH_SIZE
    first, last = lanes64 == 0, lanes64 == PATCH_SIZE - 1
    same_patch = (
        lax.broadcasted_iota(jnp.int32, (2 * LANES, LANES), 0) % LANES // PATCH_SIZE
        == lax.broadcasted_iota(jnp.int32, (2 * LANES, LANES), 1) // PATCH_SIZE
    )
    ones = jnp.where(same_patch, 1.0, 0.0).astype(jnp.bfloat16)

    def dot(a, b):
        return jnp.dot(a, b, preferred_element_type=jnp.float32)

    for date in range(sec.shape[0]):
        phase = (base[date, 0] + base[date, 1] * across) * heights[...]
        sec_real = secbuf[date, 0].astype(jnp.float32)
        sec_imag = secbuf[date, 1].astype(jnp.float32)
        cross_real = sec_real * field[0] + sec_imag * field[1]
        cross_imag = sec_imag * field[0] - sec_real * field[1]
        cosine, sine = jnp.cos(phase), jnp.sin(phase)
        real = (cross_real * cosine + cross_imag * sine).astype(jnp.bfloat16)
        imag = (cross_imag * cosine - cross_real * sine).astype(jnp.bfloat16)
        left = []
        for g in range(groups):
            re, im = (x[:, g * LANES : (g + 1) * LANES] for x in (real, imag))
            left.append(jnp.concatenate([re, im], axis=1))
            left.append(jnp.concatenate([im, -re], axis=1))
        product = dot(jnp.concatenate(left, axis=0), into[...])
        pieces = [None] * ((groups * GROUP_STEP + SPAN_LANES - GROUP_STEP) // LANES)
        for g in range(groups):
            for k in range(SPAN_LANES // LANES):
                term = product[
                    2 * rows * g : 2 * rows * (g + 1), k * LANES : (k + 1) * LANES
                ]
                at = g * GROUP_STEP // LANES + k
                pieces[at] = term if pieces[at] is None else pieces[at] + term
        colspec = jnp.concatenate(pieces, axis=1).astype(jnp.bfloat16)
        spectrum = dot(down[...], colspec)
        parts = []
        sums = []
        for k in range(len(pieces)):
            here = spectrum[:, k * LANES : (k + 1) * LANES]
            re, im = here[:PATCH_SIZE], here[PATCH_SIZE:]
            energy = re * re + im * im
            total = energy[0:SUBLANES]
            for r in range(1, PATCH_SIZE // SUBLANES):
                total = total + energy[r * SUBLANES : (r + 1) * SUBLANES]
            sums.append(total)
            parts.append((re, im, energy))
        total = jnp.concatenate(sums, axis=0)
        high = total.astype(jnp.bfloat16)
        low = (total - high.astype(jnp.float32)).astype(jnp.bfloat16)
        means = dot(jnp.concatenate([high, low], axis=1), ones)
        weighted = []
        for k, (re, im, energy) in enumerate(parts):
            mean = jnp.sum(means[k * SUBLANES : (k + 1) * SUBLANES], axis=0, keepdims=True)
            mean = mean / float(PATCH_SIZE * PATCH_SIZE)
            tall = energy + pltpu.roll(energy, 1, 0) + pltpu.roll(energy, PATCH_SIZE - 1, 0)
            before = jnp.where(
                first, pltpu.roll(tall, LANES + 1 - PATCH_SIZE, 1), pltpu.roll(tall, 1, 1)
            )
            after = jnp.where(
                last, pltpu.roll(tall, PATCH_SIZE - 1, 1), pltpu.roll(tall, LANES - 1, 1)
            )
            smooth = (tall + before + after) * (1.0 / 9.0)
            response = jnp.sqrt((smooth + 0.1 * mean) * (1.0 / (mean + 1e-06)))
            weighted.append(
                jnp.concatenate([re * response, im * response], axis=0).astype(jnp.bfloat16)
            )
        rowback = dot(up[...], jnp.concatenate(weighted, axis=1)).astype(jnp.bfloat16)
        left = []
        for g in range(groups):
            here = rowback[:, g * GROUP_STEP : g * GROUP_STEP + SPAN_LANES]
            re, im = here[:rows], here[rows:]
            left.append(jnp.concatenate([re, im], axis=1))
            left.append(jnp.concatenate([im, -re], axis=1))
        product = dot(jnp.concatenate(left, axis=0), back[...])
        merged = product[:, :LANES] * taper[0:1, :] + product[:, LANES:] * taper[1:2, :]
        merged = merged.astype(jnp.bfloat16)
        for g in range(groups):
            for part in range(2):
                begin = (2 * g + part) * rows
                out[date, part, :, g * LANES : (g + 1) * LANES] = merged[begin : begin + rows]

    for copy in sent:
        copy.wait_send()


def per_device(
    n,
    secondary_complex_slabs,
    reference_complex_slab,
    elevation_tiles,
    baseline,
    block_terrain_tile,
    block_first_row,
    block_first_column,
    block_fraction_weights,
):
    dates, _, rows, cols = secondary_complex_slabs.shape
    assert rows == HALF and elevation_tiles.shape[1:] == (SUBLANES, cols)
    lines, line = reference_complex_slab.shape[1:]
    constants = [jnp.asarray(table) for table in tables()]
    anywhere = pl.BlockSpec(memory_space=pl.ANY)
    scalars = (
        baseline,
        block_terrain_tile.reshape(-1),
        block_first_row,
        block_first_column,
        block_fraction_weights.T,
    )
    return pl.pallas_call(
        functools.partial(kernel, n),
        out_shape=pltpu.VMEM(secondary_complex_slabs.shape, jnp.bfloat16),
        in_specs=[anywhere] * 13,
        out_specs=pl.BlockSpec(memory_space=pltpu.VMEM),
        scratch_shapes=[
            pltpu.VMEM((n * elevation_tiles.shape[0],) + elevation_tiles.shape[1:], jnp.float32),
            pltpu.VMEM(elevation_tiles.shape, jnp.float32),
            pltpu.VMEM((n, elevation_tiles.shape[0] * SUBLANES, cols), jnp.int16),
            pltpu.VMEM((n, 2, lines, line), jnp.bfloat16),
            pltpu.VMEM((2, n * lines, line), jnp.float32),
            pltpu.VMEM((rows, cols), jnp.float32),
            pltpu.VMEM(secondary_complex_slabs.shape, jnp.bfloat16),
        ]
        + [pltpu.VMEM(table.shape, table.dtype) for table in constants]
        + [pltpu.SMEM(x.shape, x.dtype) for x in scalars]
        + [
            pltpu.SemaphoreType.DMA((13,)),
            pltpu.SemaphoreType.DMA((2, n // 2)),
            pltpu.SemaphoreType.DMA((2, n)),
            pltpu.SemaphoreType.DMA((2, n // 2)),
        ],
        compiler_params=pltpu.CompilerParams(collective_id=0, has_side_effects=True),
    )(
        elevation_tiles,
        reference_complex_slab,
        secondary_complex_slabs,
        *scalars,
        *constants,
    )


def solution(mesh):
    return jax.shard_map(
        functools.partial(per_device, mesh.shape["date"]),
        mesh=mesh,
        in_specs=(
            P(("groups", "date"), None, None, None),
            P(None, ("groups", "date"), None),
            P(("groups", "date"), None, None),
            P(("groups", "date"), None),
            P("groups", None),
            P("groups"),
            P("groups"),
            P("groups", None),
        ),
        out_specs=P(("groups", "date"), None, None, None),
        check_vma=False,
    )
```

```python
import functools
import math

import jax
import jax.numpy as jnp
import ml_dtypes
import numpy as np
from jax import lax
from jax.experimental import pallas as pl
from jax.experimental.pallas import tpu as pltpu
from jax.sharding import PartitionSpec as P

PATCH_SIZE = 64
HALF = PATCH_SIZE // 2
BLOCK_LINES = 4
BLOCK_SAMPLES = 16
HEIGHT_REACH = 6.0
HEIGHT_STEPS = 32767.0
LANES = 128
SUBLANES = 8
SPAN = LANES // HALF + 1
SPAN_LANES = -(-SPAN * PATCH_SIZE // LANES) * LANES
GROUP_STEP = (SPAN - 1) * PATCH_SIZE


@functools.lru_cache(maxsize=None)
def tables():
    series = np.arange(PATCH_SIZE)
    angle = (series[:, None] * series[None, :] % PATCH_SIZE) * (2.0 * math.pi / PATCH_SIZE)
    cosine, sine = np.cos(angle), np.sin(angle)
    taper = np.sin(math.pi * (series + 0.5) / PATCH_SIZE) ** 2 / (PATCH_SIZE * PATCH_SIZE)
    into = np.zeros((2, LANES, SPAN_LANES))
    back = np.zeros((2, SPAN_LANES, 2, LANES))
    for m in range(LANES):
        block, j = divmod(m, HALF)
        for half, (q, n) in enumerate(((block, HALF + j), (block + 1, j))):
            lanes = slice(q * PATCH_SIZE, (q + 1) * PATCH_SIZE)
            into[0, m, lanes] = cosine[n]
            into[1, m, lanes] = sine[n]
            back[0, lanes, half, m] = cosine[:, n]
            back[1, lanes, half, m] = -sine[:, n]
    into = into.reshape(2 * LANES, SPAN_LANES)
    back = back.reshape(2 * SPAN_LANES, 2 * LANES)
    c, s = cosine[:, :HALF], sine[:, :HALF]
    down = np.block([[c, s], [-s, c]])
    c, s = cosine[:HALF], sine[:HALF]
    up = np.block([[c, -s], [s, c]])
    weights = np.stack([np.tile(taper[HALF:], LANES // HALF), np.tile(taper[:HALF], LANES // HALF)])
    placed = tuple(m.astype(np.float32).astype(ml_dtypes.bfloat16) for m in (into, down, up, back))
    return placed + (weights.astype(np.float32),)


def flipped(index, bits):
    result = index
    bit = 1
    while bit <= bits:
        if bits & bit:
            result = result + bit - 2 * bit * (index // bit % 2)
        bit *= 2
    return result


def kernel(
    n,
    elev, ref_in, sec, base_h, tile_h, row_h, col_h, frac_h,
    into_h, down_h, up_h, back_h, taper_h,
    out,
    tiles, elevbuf, codes, refbuf, refwide, heights, secbuf, into, down, up, back, taper,
    base, first_tile, first_row, first_col, frac,
    local_sem, send_sem, recv_sem, fwd_sem,
):
    rows, cols = sec.shape[2], sec.shape[3]
    own = elev.shape[0]
    me = lax.axis_index("date")
    partner = flipped(me, 1)
    peers = [flipped(me, 2 * k) for k in reversed(range(1, n // 2))]
    sources = peers[::-1]
    barrier = pltpu.get_barrier_semaphore()
    for peer in peers + [partner]:
        pl.semaphore_signal(
            barrier, inc=1, device_id={"date": peer}, device_id_type=pl.DeviceIdType.MESH
        )

    def slot(device):
        return codes.at[device]

    def decode(device):
        whole = codes[device].astype(jnp.int32).astype(jnp.float32)
        start = pl.multiple_of(SUBLANES + device * whole.shape[0], SUBLANES)
        for group in range(cols // LANES):
            tiles[group, pl.ds(start, whole.shape[0]), :] = whole[
                :, group * LANES : (group + 1) * LANES
            ]

    local = [
        pltpu.make_async_copy(ref_in, refbuf.at[me], local_sem.at[0]),
        pltpu.make_async_copy(elev, elevbuf, local_sem.at[1]),
        pltpu.make_async_copy(sec, secbuf, local_sem.at[2]),
        pltpu.make_async_copy(into_h, into, local_sem.at[3]),
        pltpu.make_async_copy(down_h, down, local_sem.at[4]),
        pltpu.make_async_copy(up_h, up, local_sem.at[5]),
        pltpu.make_async_copy(back_h, back, local_sem.at[6]),
        pltpu.make_async_copy(taper_h, taper, local_sem.at[7]),
        pltpu.make_async_copy(base_h, base, local_sem.at[8]),
        pltpu.make_async_copy(tile_h, first_tile, local_sem.at[9]),
        pltpu.make_async_copy(row_h, first_row, local_sem.at[10]),
        pltpu.make_async_copy(col_h, first_col, local_sem.at[11]),
        pltpu.make_async_copy(frac_h, frac, local_sem.at[12]),
    ]
    local[1].start()
    for copy in local[8:] + local[:1] + local[2:8]:
        copy.start()

    def remote(src, dst, sends, number, kind, source, device):
        return pltpu.make_async_remote_copy(
            src_ref=src,
            dst_ref=dst,
            send_sem=sends.at[kind, number],
            recv_sem=recv_sem.at[kind, source],
            device_id={"date": device},
            device_id_type=pl.DeviceIdType.MESH,
        )

    local[1].wait()
    scaled = jnp.round(elevbuf[...].reshape(codes.shape[1:]) * (HEIGHT_STEPS / HEIGHT_REACH))
    codes[me] = scaled.astype(jnp.int32).astype(jnp.int16)
    pl.semaphore_wait(barrier, n // 2)
    sent = []
    for kind in (1, 0):
        for number, peer in enumerate(peers + [partner]):
            src, dst = (slot(me), slot(me)) if kind else (ref_in, refbuf.at[me])
            sent.append(remote(src, dst, send_sem, number, kind, me, peer))
            sent[-1].start()
    for kind in (1, 0):
        for number, source in enumerate(sources):
            where = slot(source) if kind else refbuf.at[source]
            copy = remote(where, where, fwd_sem, number, kind, source, partner)
            copy.wait_recv()
            copy.start()
            sent.append(copy)
        if kind:
            for device in [me] + sources:
                decode(device)
    others = [partner] + [flipped(source, 1) for source in sources]
    for copy in local[:1] + local[2:]:
        copy.wait()
    for source in others:
        remote(slot(source), slot(source), send_sem, 0, 1, source, partner).wait_recv()
        decode(source)

    lane = lax.broadcasted_iota(jnp.int32, (SUBLANES, LANES), 1)
    sublane = lax.broadcasted_iota(jnp.int32, (SUBLANES, LANES), 0)
    grid_cols = cols // BLOCK_SAMPLES
    per_group = LANES // BLOCK_SAMPLES
    bands = SUBLANES // BLOCK_LINES

    def eight_rows(step, carry):
        for group in range(cols // LANES):
            total = jnp.zeros((SUBLANES, LANES), jnp.float32)
            for band in range(bands):
                for place in range(per_group):
                    b = (step * bands + band) * grid_cols + group * per_group + place
                    tile, col = first_tile[b], first_col[b]
                    fy = frac[0, b].astype(jnp.float32)
                    fx = frac[1, b].astype(jnp.float32)
                    top = (tile + 1) * SUBLANES + first_row[b] - band * BLOCK_LINES
                    upper = tiles[0, pl.ds(top, SUBLANES), :]
                    lower = tiles[0, pl.ds(top + 1, SUBLANES), :]
                    for other in range(1, cols // LANES):
                        near = lane + (other - 1) * LANES >= col
                        upper = jnp.where(near, upper, tiles[other, pl.ds(top, SUBLANES), :])
                        lower = jnp.where(near, lower, tiles[other, pl.ds(top + 1, SUBLANES), :])
                    mixed = 16.0 * upper + fy * (lower - upper)
                    shift = place * BLOCK_SAMPLES + cols - col
                    left = pltpu.roll(mixed, (shift) & (LANES - 1), 1)
                    right = pltpu.roll(mixed, (shift - 1) & (LANES - 1), 1)
                    value = 16.0 * left + fx * (right - left)
                    inside = (lane // BLOCK_SAMPLES == place) & (sublane // BLOCK_LINES == band)
                    total = jnp.where(inside, value, total)
            heights[
                pl.ds(pl.multiple_of(step * SUBLANES, SUBLANES), SUBLANES),
                group * LANES : (group + 1) * LANES,
            ] = total * (HEIGHT_REACH / HEIGHT_STEPS / 256.0)
        return carry

    lax.fori_loop(0, rows // SUBLANES, eight_rows, 0, unroll=True)

    for source in others:
        remote(refbuf.at[source], refbuf.at[source], send_sem, 0, 0, source, partner).wait_recv()
    line = refbuf.shape[3]
    per_row = cols // line
    field = []
    for part in range(2):
        refwide[part] = refbuf[:, part].astype(jnp.float32).reshape(rows * per_row, line)
        field.append(
            jnp.concatenate(
                [refwide[part, pl.ds(m, rows, stride=per_row), :] for m in range(per_row)], axis=1
            )
        )
    lane_row = lax.broadcasted_iota(jnp.int32, (1, cols), 1).astype(jnp.float32)
    across = (lane_row + 0.5) / cols - 0.5

    groups = cols // LANES
    lanes64 = lax.broadcasted_iota(jnp.int32, (PATCH_SIZE, LANES), 1) % PATCH_SIZE
    first, last = lanes64 == 0, lanes64 == PATCH_SIZE - 1
    same_patch = (
        lax.broadcasted_iota(jnp.int32, (2 * LANES, LANES), 0) % LANES // PATCH_SIZE
        == lax.broadcasted_iota(jnp.int32, (2 * LANES, LANES), 1) // PATCH_SIZE
    )
    ones = jnp.where(same_patch, 1.0, 0.0).astype(jnp.bfloat16)

    def dot(a, b):
        return jnp.dot(a, b, preferred_element_type=jnp.float32)

    for date in range(sec.shape[0]):
        phase = (base[date, 0] + base[date, 1] * across) * heights[...]
        sec_real = secbuf[date, 0].astype(jnp.float32)
        sec_imag = secbuf[date, 1].astype(jnp.float32)
        cross_real = sec_real * field[0] + sec_imag * field[1]
        cross_imag = sec_imag * field[0] - sec_real * field[1]
        cosine, sine = jnp.cos(phase), jnp.sin(phase)
        real = (cross_real * cosine + cross_imag * sine).astype(jnp.bfloat16)
        imag = (cross_imag * cosine - cross_real * sine).astype(jnp.bfloat16)
        left = []
        for g in range(groups):
            re, im = (x[:, g * LANES : (g + 1) * LANES] for x in (real, imag))
            left.append(jnp.concatenate([re, im], axis=1))
            left.append(jnp.concatenate([im, -re], axis=1))
        product = dot(jnp.concatenate(left, axis=0), into[...])
        pieces = [None] * ((groups * GROUP_STEP + SPAN_LANES - GROUP_STEP) // LANES)
        for g in range(groups):
            for k in range(SPAN_LANES // LANES):
                term = product[
                    2 * rows * g : 2 * rows * (g + 1), k * LANES : (k + 1) * LANES
                ]
                at = g * GROUP_STEP // LANES + k
                pieces[at] = term if pieces[at] is None else pieces[at] + term
        colspec = jnp.concatenate(pieces, axis=1).astype(jnp.bfloat16)
        spectrum = dot(down[...], colspec)
        parts = []
        sums = []
        for k in range(len(pieces)):
            here = spectrum[:, k * LANES : (k + 1) * LANES]
            re, im = here[:PATCH_SIZE], here[PATCH_SIZE:]
            energy = re * re + im * im
            total = energy[0:SUBLANES]
            for r in range(1, PATCH_SIZE // SUBLANES):
                total = total + energy[r * SUBLANES : (r + 1) * SUBLANES]
            sums.append(total)
            parts.append((re, im, energy))
        total = jnp.concatenate(sums, axis=0)
        high = total.astype(jnp.bfloat16)
        low = (total - high.astype(jnp.float32)).astype(jnp.bfloat16)
        means = dot(jnp.concatenate([high, low], axis=1), ones)
        weighted = []
        for k, (re, im, energy) in enumerate(parts):
            mean = jnp.sum(means[k * SUBLANES : (k + 1) * SUBLANES], axis=0, keepdims=True)
            mean = mean / float(PATCH_SIZE * PATCH_SIZE)
            tall = energy + pltpu.roll(energy, 1, 0) + pltpu.roll(energy, PATCH_SIZE - 1, 0)
            before = jnp.where(
                first, pltpu.roll(tall, LANES + 1 - PATCH_SIZE, 1), pltpu.roll(tall, 1, 1)
            )
            after = jnp.where(
                last, pltpu.roll(tall, PATCH_SIZE - 1, 1), pltpu.roll(tall, LANES - 1, 1)
            )
            smooth = (tall + before + after) * (1.0 / 9.0)
            response = jnp.sqrt((smooth + 0.1 * mean) * (1.0 / (mean + 1e-06)))
            weighted.append(
                jnp.concatenate([re * response, im * response], axis=0).astype(jnp.bfloat16)
            )
        rowback = dot(up[...], jnp.concatenate(weighted, axis=1)).astype(jnp.bfloat16)
        left = []
        for g in range(groups):
            here = rowback[:, g * GROUP_STEP : g * GROUP_STEP + SPAN_LANES]
            re, im = here[:rows], here[rows:]
            left.append(jnp.concatenate([re, im], axis=1))
            left.append(jnp.concatenate([im, -re], axis=1))
        product = dot(jnp.concatenate(left, axis=0), back[...])
        merged = product[:, :LANES] * taper[0:1, :] + product[:, LANES:] * taper[1:2, :]
        merged = merged.astype(jnp.bfloat16)
        for g in range(groups):
            for part in range(2):
                begin = (2 * g + part) * rows
                out[date, part, :, g * LANES : (g + 1) * LANES] = merged[begin : begin + rows]

    for copy in sent:
        copy.wait_send()


def per_device(
    n,
    secondary_complex_slabs,
    reference_complex_slab,
    elevation_tiles,
    baseline,
    block_terrain_tile,
    block_first_row,
    block_first_column,
    block_fraction_weights,
):
    dates, _, rows, cols = secondary_complex_slabs.shape
    assert rows == HALF and elevation_tiles.shape[1:] == (SUBLANES, cols)
    lines, line = reference_complex_slab.shape[1:]
    constants = [jnp.asarray(table) for table in tables()]
    anywhere = pl.BlockSpec(memory_space=pl.ANY)
    scalars = (
        baseline,
        block_terrain_tile.reshape(-1),
        block_first_row,
        block_first_column,
        block_fraction_weights.T,
    )
    return pl.pallas_call(
        functools.partial(kernel, n),
        out_shape=pltpu.VMEM(secondary_complex_slabs.shape, jnp.bfloat16),
        in_specs=[anywhere] * 13,
        out_specs=pl.BlockSpec(memory_space=pltpu.VMEM),
        scratch_shapes=[
            pltpu.VMEM(
                (cols // LANES, (n * elevation_tiles.shape[0] + 2) * SUBLANES, LANES), jnp.float32
            ),
            pltpu.VMEM(elevation_tiles.shape, jnp.float32),
            pltpu.VMEM((n, elevation_tiles.shape[0] * SUBLANES, cols), jnp.int16),
            pltpu.VMEM((n, 2, lines, line), jnp.bfloat16),
            pltpu.VMEM((2, n * lines, line), jnp.float32),
            pltpu.VMEM((rows, cols), jnp.float32),
            pltpu.VMEM(secondary_complex_slabs.shape, jnp.bfloat16),
        ]
        + [pltpu.VMEM(table.shape, table.dtype) for table in constants]
        + [pltpu.SMEM(x.shape, x.dtype) for x in scalars]
        + [
            pltpu.SemaphoreType.DMA((13,)),
            pltpu.SemaphoreType.DMA((2, n // 2)),
            pltpu.SemaphoreType.DMA((2, n)),
            pltpu.SemaphoreType.DMA((2, n // 2)),
        ],
        compiler_params=pltpu.CompilerParams(collective_id=0, has_side_effects=True),
    )(
        elevation_tiles,
        reference_complex_slab,
        secondary_complex_slabs,
        *scalars,
        *constants,
    )


def solution(mesh):
    return jax.shard_map(
        functools.partial(per_device, mesh.shape["date"]),
        mesh=mesh,
        in_specs=(
            P(("groups", "date"), None, None, None),
            P(None, ("groups", "date"), None),
            P(("groups", "date"), None, None),
            P(("groups", "date"), None),
            P("groups", None),
            P("groups"),
            P("groups"),
            P("groups", None),
        ),
        out_specs=P(("groups", "date"), None, None, None),
        check_vma=False,
    )
```

```python
import functools
import math

import jax
import jax.numpy as jnp
import ml_dtypes
import numpy as np
from jax import lax
from jax.experimental import pallas as pl
from jax.experimental.pallas import tpu as pltpu
from jax.sharding import PartitionSpec as P

PATCH_SIZE = 64
HALF = PATCH_SIZE // 2
BLOCK_LINES = 4
BLOCK_SAMPLES = 16
HEIGHT_REACH = 6.0
HEIGHT_STEPS = 32767.0
LANES = 128
SUBLANES = 8
SPAN = LANES // HALF + 1
SPAN_LANES = -(-SPAN * PATCH_SIZE // LANES) * LANES
GROUP_STEP = (SPAN - 1) * PATCH_SIZE


@functools.lru_cache(maxsize=None)
def tables():
    series = np.arange(PATCH_SIZE)
    angle = (series[:, None] * series[None, :] % PATCH_SIZE) * (2.0 * math.pi / PATCH_SIZE)
    cosine, sine = np.cos(angle), np.sin(angle)
    taper = np.sin(math.pi * (series + 0.5) / PATCH_SIZE) ** 2 / (PATCH_SIZE * PATCH_SIZE)
    into = np.zeros((2, LANES, SPAN_LANES))
    back = np.zeros((2, SPAN_LANES, 2, LANES))
    for m in range(LANES):
        block, j = divmod(m, HALF)
        for half, (q, n) in enumerate(((block, HALF + j), (block + 1, j))):
            lanes = slice(q * PATCH_SIZE, (q + 1) * PATCH_SIZE)
            into[0, m, lanes] = cosine[n]
            into[1, m, lanes] = sine[n]
            back[0, lanes, half, m] = cosine[:, n]
            back[1, lanes, half, m] = -sine[:, n]
    into = into.reshape(2 * LANES, SPAN_LANES)
    back = back.reshape(2 * SPAN_LANES, 2 * LANES)
    c, s = cosine[:, :HALF], sine[:, :HALF]
    down = np.block([[c, s], [-s, c]])
    c, s = cosine[:HALF], sine[:HALF]
    up = np.block([[c, -s], [s, c]])
    weights = np.stack([np.tile(taper[HALF:], LANES // HALF), np.tile(taper[:HALF], LANES // HALF)])
    placed = tuple(m.astype(np.float32).astype(ml_dtypes.bfloat16) for m in (into, down, up, back))
    return placed + (weights.astype(np.float32),)


def flipped(index, bits):
    result = index
    bit = 1
    while bit <= bits:
        if bits & bit:
            result = result + bit - 2 * bit * (index // bit % 2)
        bit *= 2
    return result


def kernel(
    n,
    elev, ref_in, sec, base_h, tile_h, row_h, col_h, frac_h,
    into_h, down_h, up_h, back_h, taper_h,
    out,
    tiles, elevbuf, codes, refbuf, refwide, heights, secbuf, into, down, up, back, taper,
    base, first_tile, first_row, first_col, frac,
    local_sem, send_sem, recv_sem, fwd_sem,
):
    rows, cols = sec.shape[2], sec.shape[3]
    own = elev.shape[0]
    me = lax.axis_index("date")
    partner = flipped(me, 1)
    peers = [flipped(me, 2 * k) for k in reversed(range(1, n // 2))]
    sources = peers[::-1]
    elev_copy = pltpu.make_async_copy(elev, elevbuf, local_sem.at[1])
    elev_copy.start()
    barrier = pltpu.get_barrier_semaphore()
    for peer in peers + [partner]:
        pl.semaphore_signal(
            barrier, inc=1, device_id={"date": peer}, device_id_type=pl.DeviceIdType.MESH
        )

    def slot(device):
        return codes.at[device]

    def decode(device):
        whole = codes[device].astype(jnp.int32).astype(jnp.float32)
        start = pl.multiple_of(SUBLANES + device * whole.shape[0], SUBLANES)
        for group in range(cols // LANES):
            tiles[group, pl.ds(start, whole.shape[0]), :] = whole[
                :, group * LANES : (group + 1) * LANES
            ]

    local = [
        pltpu.make_async_copy(ref_in, refbuf.at[me], local_sem.at[0]),
        elev_copy,
        pltpu.make_async_copy(sec, secbuf, local_sem.at[2]),
        pltpu.make_async_copy(into_h, into, local_sem.at[3]),
        pltpu.make_async_copy(down_h, down, local_sem.at[4]),
        pltpu.make_async_copy(up_h, up, local_sem.at[5]),
        pltpu.make_async_copy(back_h, back, local_sem.at[6]),
        pltpu.make_async_copy(taper_h, taper, local_sem.at[7]),
        pltpu.make_async_copy(base_h, base, local_sem.at[8]),
        pltpu.make_async_copy(tile_h, first_tile, local_sem.at[9]),
        pltpu.make_async_copy(row_h, first_row, local_sem.at[10]),
        pltpu.make_async_copy(col_h, first_col, local_sem.at[11]),
        pltpu.make_async_copy(frac_h, frac, local_sem.at[12]),
    ]
    for copy in local[:1]:
        copy.start()

    def remote(src, dst, sends, number, kind, source, device):
        return pltpu.make_async_remote_copy(
            src_ref=src,
            dst_ref=dst,
            send_sem=sends.at[kind, number],
            recv_sem=recv_sem.at[kind, source],
            device_id={"date": device},
            device_id_type=pl.DeviceIdType.MESH,
        )

    local[1].wait()
    scaled = jnp.round(elevbuf[...].reshape(codes.shape[1:]) * (HEIGHT_STEPS / HEIGHT_REACH))
    codes[me] = scaled.astype(jnp.int32).astype(jnp.int16)
    pl.semaphore_wait(barrier, n // 2)
    sent = []
    for kind in (1, 0):
        for number, peer in enumerate(peers + [partner]):
            src, dst = (slot(me), slot(me)) if kind else (ref_in, refbuf.at[me])
            sent.append(remote(src, dst, send_sem, number, kind, me, peer))
            sent[-1].start()
    for copy in local[8:] + local[2:8]:
        copy.start()
    for kind in (1, 0):
        for number, source in enumerate(sources):
            where = slot(source) if kind else refbuf.at[source]
            copy = remote(where, where, fwd_sem, number, kind, source, partner)
            copy.wait_recv()
            copy.start()
            sent.append(copy)
        if kind:
            for device in [me] + sources:
                decode(device)
    others = [partner] + [flipped(source, 1) for source in sources]
    for copy in local[:1] + local[2:]:
        copy.wait()
    for source in others:
        remote(slot(source), slot(source), send_sem, 0, 1, source, partner).wait_recv()
        decode(source)

    lane = lax.broadcasted_iota(jnp.int32, (SUBLANES, LANES), 1)
    sublane = lax.broadcasted_iota(jnp.int32, (SUBLANES, LANES), 0)
    grid_cols = cols // BLOCK_SAMPLES
    per_group = LANES // BLOCK_SAMPLES
    bands = SUBLANES // BLOCK_LINES

    def eight_rows(step, carry):
        for group in range(cols // LANES):
            total = jnp.zeros((SUBLANES, LANES), jnp.float32)
            for band in range(bands):
                for place in range(per_group):
                    b = (step * bands + band) * grid_cols + group * per_group + place
                    tile, col = first_tile[b], first_col[b]
                    fy = frac[0, b].astype(jnp.float32)
                    fx = frac[1, b].astype(jnp.float32)
                    top = (tile + 1) * SUBLANES + first_row[b] - band * BLOCK_LINES
                    upper = tiles[0, pl.ds(top, SUBLANES), :]
                    lower = tiles[0, pl.ds(top + 1, SUBLANES), :]
                    for other in range(1, cols // LANES):
                        near = lane + (other - 1) * LANES >= col
                        upper = jnp.where(near, upper, tiles[other, pl.ds(top, SUBLANES), :])
                        lower = jnp.where(near, lower, tiles[other, pl.ds(top + 1, SUBLANES), :])
                    mixed = 16.0 * upper + fy * (lower - upper)
                    shift = place * BLOCK_SAMPLES + cols - col
                    left = pltpu.roll(mixed, (shift) & (LANES - 1), 1)
                    right = pltpu.roll(mixed, (shift - 1) & (LANES - 1), 1)
                    value = 16.0 * left + fx * (right - left)
                    inside = (lane // BLOCK_SAMPLES == place) & (sublane // BLOCK_LINES == band)
                    total = jnp.where(inside, value, total)
            heights[
                pl.ds(pl.multiple_of(step * SUBLANES, SUBLANES), SUBLANES),
                group * LANES : (group + 1) * LANES,
            ] = total * (HEIGHT_REACH / HEIGHT_STEPS / 256.0)
        return carry

    lax.fori_loop(0, rows // SUBLANES, eight_rows, 0, unroll=True)

    for source in others:
        remote(refbuf.at[source], refbuf.at[source], send_sem, 0, 0, source, partner).wait_recv()
    line = refbuf.shape[3]
    per_row = cols // line
    field = []
    for part in range(2):
        refwide[part] = refbuf[:, part].astype(jnp.float32).reshape(rows * per_row, line)
        field.append(
            jnp.concatenate(
                [refwide[part, pl.ds(m, rows, stride=per_row), :] for m in range(per_row)], axis=1
            )
        )
    lane_row = lax.broadcasted_iota(jnp.int32, (1, cols), 1).astype(jnp.float32)
    across = (lane_row + 0.5) / cols - 0.5

    groups = cols // LANES
    lanes64 = lax.broadcasted_iota(jnp.int32, (PATCH_SIZE, LANES), 1) % PATCH_SIZE
    first, last = lanes64 == 0, lanes64 == PATCH_SIZE - 1
    same_patch = (
        lax.broadcasted_iota(jnp.int32, (2 * LANES, LANES), 0) % LANES // PATCH_SIZE
        == lax.broadcasted_iota(jnp.int32, (2 * LANES, LANES), 1) // PATCH_SIZE
    )
    ones = jnp.where(same_patch, 1.0, 0.0).astype(jnp.bfloat16)

    def dot(a, b):
        return jnp.dot(a, b, preferred_element_type=jnp.float32)

    for date in range(sec.shape[0]):
        phase = (base[date, 0] + base[date, 1] * across) * heights[...]
        sec_real = secbuf[date, 0].astype(jnp.float32)
        sec_imag = secbuf[date, 1].astype(jnp.float32)
        cross_real = sec_real * field[0] + sec_imag * field[1]
        cross_imag = sec_imag * field[0] - sec_real * field[1]
        cosine, sine = jnp.cos(phase), jnp.sin(phase)
        real = (cross_real * cosine + cross_imag * sine).astype(jnp.bfloat16)
        imag = (cross_imag * cosine - cross_real * sine).astype(jnp.bfloat16)
        left = []
        for g in range(groups):
            re, im = (x[:, g * LANES : (g + 1) * LANES] for x in (real, imag))
            left.append(jnp.concatenate([re, im], axis=1))
            left.append(jnp.concatenate([im, -re], axis=1))
        product = dot(jnp.concatenate(left, axis=0), into[...])
        pieces = [None] * ((groups * GROUP_STEP + SPAN_LANES - GROUP_STEP) // LANES)
        for g in range(groups):
            for k in range(SPAN_LANES // LANES):
                term = product[
                    2 * rows * g : 2 * rows * (g + 1), k * LANES : (k + 1) * LANES
                ]
                at = g * GROUP_STEP // LANES + k
                pieces[at] = term if pieces[at] is None else pieces[at] + term
        colspec = jnp.concatenate(pieces, axis=1).astype(jnp.bfloat16)
        spectrum = dot(down[...], colspec)
        parts = []
        sums = []
        for k in range(len(pieces)):
            here = spectrum[:, k * LANES : (k + 1) * LANES]
            re, im = here[:PATCH_SIZE], here[PATCH_SIZE:]
            energy = re * re + im * im
            total = energy[0:SUBLANES]
            for r in range(1, PATCH_SIZE // SUBLANES):
                total = total + energy[r * SUBLANES : (r + 1) * SUBLANES]
            sums.append(total)
            parts.append((re, im, energy))
        total = jnp.concatenate(sums, axis=0)
        high = total.astype(jnp.bfloat16)
        low = (total - high.astype(jnp.float32)).astype(jnp.bfloat16)
        means = dot(jnp.concatenate([high, low], axis=1), ones)
        weighted = []
        for k, (re, im, energy) in enumerate(parts):
            mean = jnp.sum(means[k * SUBLANES : (k + 1) * SUBLANES], axis=0, keepdims=True)
            mean = mean / float(PATCH_SIZE * PATCH_SIZE)
            tall = energy + pltpu.roll(energy, 1, 0) + pltpu.roll(energy, PATCH_SIZE - 1, 0)
            before = jnp.where(
                first, pltpu.roll(tall, LANES + 1 - PATCH_SIZE, 1), pltpu.roll(tall, 1, 1)
            )
            after = jnp.where(
                last, pltpu.roll(tall, PATCH_SIZE - 1, 1), pltpu.roll(tall, LANES - 1, 1)
            )
            smooth = (tall + before + after) * (1.0 / 9.0)
            response = jnp.sqrt((smooth + 0.1 * mean) * (1.0 / (mean + 1e-06)))
            weighted.append(
                jnp.concatenate([re * response, im * response], axis=0).astype(jnp.bfloat16)
            )
        rowback = dot(up[...], jnp.concatenate(weighted, axis=1)).astype(jnp.bfloat16)
        left = []
        for g in range(groups):
            here = rowback[:, g * GROUP_STEP : g * GROUP_STEP + SPAN_LANES]
            re, im = here[:rows], here[rows:]
            left.append(jnp.concatenate([re, im], axis=1))
            left.append(jnp.concatenate([im, -re], axis=1))
        product = dot(jnp.concatenate(left, axis=0), back[...])
        merged = product[:, :LANES] * taper[0:1, :] + product[:, LANES:] * taper[1:2, :]
        merged = merged.astype(jnp.bfloat16)
        for g in range(groups):
            for part in range(2):
                begin = (2 * g + part) * rows
                out[date, part, :, g * LANES : (g + 1) * LANES] = merged[begin : begin + rows]

    for copy in sent:
        copy.wait_send()


def per_device(
    n,
    secondary_complex_slabs,
    reference_complex_slab,
    elevation_tiles,
    baseline,
    block_terrain_tile,
    block_first_row,
    block_first_column,
    block_fraction_weights,
):
    dates, _, rows, cols = secondary_complex_slabs.shape
    assert rows == HALF and elevation_tiles.shape[1:] == (SUBLANES, cols)
    lines, line = reference_complex_slab.shape[1:]
    constants = [jnp.asarray(table) for table in tables()]
    anywhere = pl.BlockSpec(memory_space=pl.ANY)
    scalars = (
        baseline,
        block_terrain_tile.reshape(-1),
        block_first_row,
        block_first_column,
        block_fraction_weights.T,
    )
    return pl.pallas_call(
        functools.partial(kernel, n),
        out_shape=pltpu.VMEM(secondary_complex_slabs.shape, jnp.bfloat16),
        in_specs=[anywhere] * 13,
        out_specs=pl.BlockSpec(memory_space=pltpu.VMEM),
        scratch_shapes=[
            pltpu.VMEM(
                (cols // LANES, (n * elevation_tiles.shape[0] + 2) * SUBLANES, LANES), jnp.float32
            ),
            pltpu.VMEM(elevation_tiles.shape, jnp.float32),
            pltpu.VMEM((n, elevation_tiles.shape[0] * SUBLANES, cols), jnp.int16),
            pltpu.VMEM((n, 2, lines, line), jnp.bfloat16),
            pltpu.VMEM((2, n * lines, line), jnp.float32),
            pltpu.VMEM((rows, cols), jnp.float32),
            pltpu.VMEM(secondary_complex_slabs.shape, jnp.bfloat16),
        ]
        + [pltpu.VMEM(table.shape, table.dtype) for table in constants]
        + [pltpu.SMEM(x.shape, x.dtype) for x in scalars]
        + [
            pltpu.SemaphoreType.DMA((13,)),
            pltpu.SemaphoreType.DMA((2, n // 2)),
            pltpu.SemaphoreType.DMA((2, n)),
            pltpu.SemaphoreType.DMA((2, n // 2)),
        ],
        compiler_params=pltpu.CompilerParams(collective_id=0, has_side_effects=True),
    )(
        elevation_tiles,
        reference_complex_slab,
        secondary_complex_slabs,
        *scalars,
        *constants,
    )


def solution(mesh):
    return jax.shard_map(
        functools.partial(per_device, mesh.shape["date"]),
        mesh=mesh,
        in_specs=(
            P(("groups", "date"), None, None, None),
            P(None, ("groups", "date"), None),
            P(("groups", "date"), None, None),
            P(("groups", "date"), None),
            P("groups", None),
            P("groups"),
            P("groups"),
            P("groups", None),
        ),
        out_specs=P(("groups", "date"), None, None, None),
        check_vma=False,
    )
```
